32 devices in a mesh: row: 2 (over x), col: 4 (over z), depth: 4 (over y, core).
Axes of the slice: x: 2, y: 2, z: 4, core: 2. Of those that a mesh axis runs over, the one named last changes fastest.
Arguments:
- alignment_matrix: bfloat16 [128, 384, 256], P('depth', 'col'), may hold values from -6 to 6
- twin_linear_matrix: bfloat16 [256, 64], replicated, may hold values from -0.375 to 0.375
- final_matrix: bfloat16 [1024, 128], replicated, may hold values from -2 to 2
- final_offset: float32 [128], replicated, may hold values from -3 to 3
- adjoint_incoming: bfloat16 [384, 384, 128], P('row', ('col', 'depth')), may hold values from -6 to 6
Outputs:
- contact_delta: bfloat16 [384, 384, 128], P('row', ('col', 'depth'))
- alignment_adjoint: float32 [128, 384, 256], P('depth', 'col')
- grad_w_out: float32 [1024, 128], replicated
- grad_b_out: float32 [128], replicated
The draws below stay inside these ranges and needn't reach their ends.
All inputs are finite; a program needn't handle non-finite values.
Results may differ from the reference program's by a relative error of at most 0.007.
Values may be sent and summed in bfloat16 or wider, within the bound.
A program may use at most 128 MiB of HBM per device.

```python
import jax
import jax.numpy as jnp
from jax import lax

ALIGN_FEATURES = 256
HIDDEN_CHANNELS = 32
CONTACT_FEATURES = 128
RES = 96
ALIGNMENT_ROWS = 128
KRONECKER_SIZE = 1024
AMINO_ACID_COUNT = 384


def block_levels(own_key, shape, shards, least, high):
    def one(dim, blocks):
        heights = jax.random.uniform(jax.random.fold_in(jax.random.fold_in(own_key, 6), dim), (blocks,), jnp.float32, least / len(shards), high / len(shards))
        return jnp.repeat(jnp.exp(heights), shape[dim] // blocks).reshape((-1,) + (1,) * (len(shape) - dim - 1))

    loudness = one(*shards[0])
    for cut in shards[1:]:
        loudness = loudness * one(*cut)
    return loudness


def scatter_about(key, extent, width, bound, split=(), kind=jnp.bfloat16):
    result = width * jax.random.normal(key, extent, jnp.float32)
    if split:
        result = result * block_levels(key, extent, split, -0.22, 0.18)
    return jnp.clip(result, -bound, bound).astype(kind)


def setup_inputs(seed: int = 0) -> dict:
    key_of = jax.random.split(jax.random.key(seed), 6)
    alignment_matrix = scatter_about(key_of[0], (ALIGNMENT_ROWS, AMINO_ACID_COUNT, ALIGN_FEATURES), 1.0, 6.0, ((0, 4), (1, 4)))
    twin_linear_matrix = scatter_about(key_of[1], (ALIGN_FEATURES, 2 * HIDDEN_CHANNELS), ALIGN_FEATURES ** -0.5, 0.375)
    final_matrix = scatter_about(key_of[2], (KRONECKER_SIZE, CONTACT_FEATURES), (KRONECKER_SIZE // ALIGNMENT_ROWS) ** -0.5, 2.0)
    final_offset = scatter_about(key_of[3], (CONTACT_FEATURES,), 0.5, 3.0, (), jnp.float32)
    adjoint_incoming = scatter_about(key_of[4], (AMINO_ACID_COUNT, AMINO_ACID_COUNT, CONTACT_FEATURES), 1.0, 6.0, ((0, 2), (1, 16)))
    return {"alignment_matrix": alignment_matrix, "twin_linear_matrix": twin_linear_matrix, "final_matrix": final_matrix, "final_offset": final_offset, "adjoint_incoming": adjoint_incoming}


epsilon = 1e-05

def standardize_channels(values):
    centre = lax.optimization_barrier(jnp.mean(values, axis=-1, keepdims=True))
    spread = lax.optimization_barrier(jnp.mean(jnp.square(values - centre), axis=-1, keepdims=True))
    return (values - centre) * lax.rsqrt(spread + epsilon)

def reference(alignment_matrix, twin_linear_matrix, final_matrix, final_offset, adjoint_incoming):
    latent_features = twin_linear_matrix.shape[1] // 2
    standardized_alignment, standardize_backprop = jax.vjp(standardize_channels, alignment_matrix.astype(jnp.float32))
    normed = standardized_alignment.astype(jnp.bfloat16)
    panels = jnp.dot(normed, twin_linear_matrix, preferred_element_type=jnp.float32).astype(jnp.bfloat16)
    left = panels[..., :latent_features].astype(jnp.float32)
    right = panels[..., latent_features:].astype(jnp.float32)
    blocks = AMINO_ACID_COUNT // RES

    def one_block(state_acc, step_index):
        matrix_accumulator, offset_accumulator, right_acc = state_acc
        offset = (step_index * RES).astype(jnp.int32)
        rows_left = lax.dynamic_slice_in_dim(left, offset, RES, 1)
        kronecker_tile = jnp.einsum('sic,sje->ijce', rows_left, right).reshape(RES, AMINO_ACID_COUNT, KRONECKER_SIZE)
        kronecker_tile = (kronecker_tile / ALIGNMENT_ROWS).astype(jnp.bfloat16)
        pair_blk = (jnp.dot(kronecker_tile, final_matrix, preferred_element_type=jnp.float32) + final_offset).astype(jnp.bfloat16)
        adjoint_tile = lax.dynamic_slice_in_dim(adjoint_incoming, offset, RES, 0).astype(jnp.float32)
        adjoint_kronecker = (jnp.einsum('gtz,vz->gtv', adjoint_tile, final_matrix.astype(jnp.float32)) / ALIGNMENT_ROWS).astype(jnp.bfloat16)
        grad_four = adjoint_kronecker.astype(jnp.float32).reshape(RES, AMINO_ACID_COUNT, latent_features, latent_features)
        left_blk = jnp.einsum('ijce,sje->sic', grad_four, right)
        right_acc = right_acc + jnp.einsum('ijce,sic->sje', grad_four, rows_left)
        matrix_accumulator = matrix_accumulator + jnp.einsum('ijf,ijo->fo', kronecker_tile.astype(jnp.float32), adjoint_tile)
        offset_accumulator = offset_accumulator + lax.optimization_barrier(jnp.sum(adjoint_tile, axis=(0, 1)))
        return ((matrix_accumulator, offset_accumulator, right_acc), (pair_blk, left_blk))
    initial_carry = (jnp.zeros((KRONECKER_SIZE, CONTACT_FEATURES), jnp.float32), jnp.zeros((CONTACT_FEATURES,), jnp.float32), jnp.zeros((ALIGNMENT_ROWS, AMINO_ACID_COUNT, latent_features), jnp.float32))
    final_state, stacked = lax.scan(one_block, initial_carry, jnp.arange(blocks, dtype=jnp.int32))
    matrix_accumulator, offset_accumulator, right_acc = final_state
    pair_blocks, leftside_tiles = stacked
    contact_delta = pair_blocks.reshape(AMINO_ACID_COUNT, AMINO_ACID_COUNT, CONTACT_FEATURES)
    adjoint_leftside = jnp.transpose(leftside_tiles, (1, 0, 2, 3)).reshape(ALIGNMENT_ROWS, AMINO_ACID_COUNT, latent_features)
    grad_panels = jnp.concatenate([adjoint_leftside, right_acc], axis=-1).astype(jnp.bfloat16)
    standardized_adjoint = jnp.dot(grad_panels, jnp.transpose(twin_linear_matrix), preferred_element_type=jnp.float32)
    alignment_adjoint = standardize_backprop(standardized_adjoint)[0]
    return (contact_delta, alignment_adjoint, matrix_accumulator / AMINO_ACID_COUNT, offset_accumulator / AMINO_ACID_COUNT)
```

```python
import functools

import jax
import jax.numpy as jnp
from jax import lax
from jax.experimental import pallas as pl
from jax.experimental.pallas import tpu as pltpu
from jax.sharding import PartitionSpec as P

epsilon = 1e-05
MESH = pl.DeviceIdType.MESH
F32 = jnp.float32
BF16 = jnp.bfloat16


def standardize_channels(values):
    centre = jnp.mean(values, axis=-1, keepdims=True)
    spread = jnp.mean(jnp.square(values - centre), axis=-1, keepdims=True)
    return (values - centre) * lax.rsqrt(spread + epsilon)


def remote(src, dst, send, recv, where):
    return pltpu.make_async_remote_copy(
        src_ref=src, dst_ref=dst, send_sem=send, recv_sem=recv, device_id=where, device_id_type=MESH
    )


def lanes(start, size):
    return pl.ds(pl.multiple_of(start, 128), size)


def rows(start, size):
    return pl.ds(pl.multiple_of(start, size), size)


def gather_kernel(R, C, D, lt, rt, L, rout, Z, zs, zr, xs, xr, ps, pr, rs, rr, lsem):
    r, c, d = lax.axis_index("row"), lax.axis_index("col"), lax.axis_index("depth")
    NI, W = lt.shape
    H = W // R
    ratio = C // R
    barrier = pltpu.get_barrier_semaphore()
    count = 0
    for k in range(1, C):
        pl.semaphore_signal(barrier, inc=1, device_id=(r, lax.rem(c + k, C), d), device_id_type=MESH)
        count += 1
    for k in range(1, R):
        pl.semaphore_signal(barrier, inc=1, device_id=(lax.rem(r + k, R), c, d), device_id_type=MESH)
        count += 1
    for k in range(1, D):
        pl.semaphore_signal(barrier, inc=1, device_id=(r, c, lax.rem(d + k, D)), device_id_type=MESH)
        count += 1
    pl.semaphore_wait(barrier, count)
    started = []
    mine = lt.at[:, lanes(r * H, H)]
    own = pltpu.make_async_copy(mine, Z.at[c], zr.at[0])
    own.start()
    for k in range(1, C):
        cp = remote(mine, Z.at[c], zs.at[k], zr.at[k], (r, lax.rem(c + k, C), d))
        cp.start()
        started.append(cp)
    ownr = pltpu.make_async_copy(rt.at[d], rout.at[d], rs.at[0])
    ownr.start()
    for k in range(1, D):
        t = lax.rem(d + k, D)
        cp = remote(rt.at[t], rout.at[d], rs.at[k], rr.at[k], (r, c, t))
        cp.start()
        started.append(cp)
    peers = range(1, D)
    pieces = []
    for m in range(R - 1, -1, -1):
        to = lax.rem(r + m, R)
        for b in range(ratio):
            block = to * ratio + b
            k = lax.rem(c - block + C, C)
            pltpu.make_async_copy(Z.at[block], Z.at[block], zr.at[k]).wait()
            where = (pl.ds(b * NI, NI), lanes(d * W + r * H, H))
            if m:
                cp = remote(Z.at[block], L.at[where], xs.at[m, b], xr.at[m, b], (to, c, d))
                cp.start()
                started.append(cp)
            else:
                cp = pltpu.make_async_copy(Z.at[block], L.at[where], lsem.at[b])
                cp.start()
                pieces.append(cp)
    hops = ((1, 2), (0, 1)) if D == 4 else tuple((k - 1, k) for k in peers)

    def peer(k):
        if D == 4 and k == 1:
            return d + 1 - 2 * lax.rem(d, 2)
        return lax.rem(d + k, D)

    def spot(b, m, who):
        return (pl.ds(b * NI, NI), lanes(who * W + lax.rem(r - m + R, R) * H, H))

    for m in range(R):
        for b in range(ratio):
            if m == 0:
                pieces[b].wait()
            else:
                at = L.at[spot(b, m, d)]
                pltpu.make_async_copy(at, at, xr.at[m, b]).wait()
            at = L.at[spot(b, m, d)]
            for slot, k in hops:
                cp = remote(at, at, ps.at[slot, m, b], pr.at[slot, m, b], (r, c, peer(k)))
                cp.start()
                started.append(cp)
    if D == 4:
        far = lax.rem(d + 2, D)
        near = peer(1)
        for m in range(R):
            for b in range(ratio):
                at = L.at[spot(b, m, far)]
                pltpu.make_async_copy(at, at, pr.at[1, m, b]).wait()
                cp = remote(at, at, ps.at[2, m, b], pr.at[2, m, b], (r, c, near))
                cp.start()
                started.append(cp)
        for m in range(R):
            for b in range(ratio):
                at = L.at[spot(b, m, near)]
                pltpu.make_async_copy(at, at, pr.at[0, m, b]).wait()
                at = L.at[spot(b, m, lax.rem(near + 2, D))]
                pltpu.make_async_copy(at, at, pr.at[2, m, b]).wait()
    else:
        for slot, k in hops:
            for m in range(R):
                for b in range(ratio):
                    at = L.at[spot(b, m, lax.rem(d - k + D, D))]
                    pltpu.make_async_copy(at, at, pr.at[slot, m, b]).wait()
    ownr.wait()
    for k in range(1, D):
        at = rout.at[lax.rem(d - k + D, D)]
        pltpu.make_async_copy(at, at, rr.at[k]).wait()
    for cp in started:
        cp.wait_send()


def pair_kernel(
    D, SL, CH, JB, S, crop, L, A, RM, RT, WF, WR, off, out, gl, gr, w, bsum, LT, T, U, acc, wacc, bacc
):
    step = pl.program_id(0)
    O = off.shape[1]
    W = CH * SL

    @pl.when(step == 0)
    def _():
        LT[...] = L[...].T
        acc[...] = jnp.zeros_like(acc)
        wacc[...] = jnp.zeros_like(wacc)
        bacc[...] = jnp.zeros_like(bacc)

    full = WF.shape[1]
    part = min(1024, full)
    for j in range(JB):
        right = RM[j * S : (j + 1) * S, :]
        for n in range(full // part):
            made = jnp.dot(right, WF[:, n * part : (n + 1) * part], preferred_element_type=F32).astype(BF16)
            for q in range(part // O):
                c = n * (part // O) + q
                for g in range(D):
                    T[g * W + c * SL : g * W + (c + 1) * SL, j * O : (j + 1) * O] = made[
                        g * SL : (g + 1) * SL, q * O : (q + 1) * O
                    ]
    offset = jnp.concatenate([off[...]] * JB, axis=1)
    out[...] = (
        jnp.dot(L[...], T[...], preferred_element_type=F32) * (1.0 / S) + offset
    ).astype(BF16)
    adj = A[...]
    for g in range(D):
        acc[:, g * W : (g + 1) * W] += lax.dot_general(
            adj, T[g * W : (g + 1) * W, :], (((1,), (1,)), ((), ())), preferred_element_type=F32
        )
        made = jnp.dot(LT[g * W : (g + 1) * W, :], adj, preferred_element_type=F32).astype(BF16)
        for c in range(CH):
            for j in range(JB):
                U[j * S + g * SL : j * S + (g + 1) * SL, c * O : (c + 1) * O] = made[
                    c * SL : (c + 1) * SL, j * O : (j + 1) * O
                ]
    gr[...] = jnp.dot(U[...], WR[...], preferred_element_type=F32) * (1.0 / S)
    wacc[...] += jnp.dot(RT[...], U[...], preferred_element_type=F32)
    total = jnp.sum(adj.astype(F32), axis=0, keepdims=True)
    for j in range(JB):
        bacc[0:1, :] += total[:, j * O : (j + 1) * O]

    @pl.when(step == pl.num_programs(0) - 1)
    def _():
        gl[...] = (acc[...] * (1.0 / S)).astype(BF16)
        w[...] = wacc[...] * (1.0 / (S * crop))
        bsum[...] = bacc[...] * (1.0 / crop)


def reduce_kernel(
    R, C, D, gl, gr, wv, glout, grout, wout, bout,
    cbuf, ysrc, ybuf, xsrc, Zp, zin, fin, grin, win, wsum,
    cs, cr, ys, yr, xs, xr, zs, zr, fs, fr, gs, grr, ws, wr, vs, vr, ls,
):
    r, c, d = lax.axis_index("row"), lax.axis_index("col"), lax.axis_index("depth")
    N = R * C * D
    me = (r * C + c) * D + d
    W = gl.shape[1] // D
    H = W // R
    ratio = C // R
    NI = gl.shape[0] // ratio

    def place(t):
        return (t // (C * D), lax.rem(t // D, C), lax.rem(t, D))

    barrier = pltpu.get_barrier_semaphore()

    def greet(k, carry):
        pl.semaphore_signal(barrier, inc=1, device_id=place(lax.rem(me + k, N)), device_id_type=MESH)
        return carry

    lax.fori_loop(1, N, greet, 0)
    pl.semaphore_wait(barrier, N - 1)
    near = d + 1 - 2 * lax.rem(d, 2)
    far = lax.rem(d + 2, D)
    nearfar = lax.rem(near + 2, D)
    started = []
    first = remote(gl.at[:, lanes(nearfar * W, W)], cbuf.at[1], cs.at[1], cr.at[1], (r, c, near))
    first.start()
    second = remote(gl.at[:, lanes(near * W, W)], cbuf.at[0], cs.at[0], cr.at[0], (r, c, near))
    second.start()
    started += [first, second]

    def spread(k, carry):
        t = lax.rem(me + k, N)
        remote(wv.at[t], win.at[me], ws, wr, place(t)).start()
        return carry

    lax.fori_loop(1, N, spread, 0)
    ownw = pltpu.make_async_copy(wv.at[me], win.at[me], ls.at[0])
    ownw.start()
    RD = R * D
    slot = r * D + d
    for k in range(1, RD):
        t = lax.rem(slot + k, RD)
        cp = remote(
            gr.at[lax.rem(t, D)], grin.at[slot], gs.at[k], grr.at[k], (t // D, c, lax.rem(t, D))
        )
        cp.start()
        started.append(cp)
    owng = pltpu.make_async_copy(gr.at[d], grin.at[slot], ls.at[1])
    owng.start()

    first.wait_recv()
    ysrc[...] = (gl[:, lanes(far * W, W)].astype(F32) + cbuf[1].astype(F32)).astype(BF16)
    ycp = remote(ysrc, ybuf, ys, yr, (r, c, far))
    ycp.start()
    started.append(ycp)
    second.wait_recv()
    ycp.wait_recv()
    for h in range(R):
        cut = slice(h * H, (h + 1) * H)
        xsrc[h] = (
            gl[:, lanes(d * W + h * H, H)].astype(F32)
            + cbuf[0, :, cut].astype(F32)
            + ybuf[:, cut].astype(F32)
        ).astype(BF16)
    ownx = pltpu.make_async_copy(xsrc.at[r], Zp.at[r], ls.at[2])
    ownx.start()
    xcps = []
    for m in range(1, R):
        to = lax.rem(r + m, R)
        cp = remote(xsrc.at[to], Zp.at[r], xs.at[m], xr.at[m], (to, c, d))
        cp.start()
        xcps.append(cp)
    started += xcps

    ownw.wait()
    pltpu.make_async_copy(win.at[pl.ds(0, N - 1)], win.at[pl.ds(0, N - 1)], wr).wait()
    share = wsum.shape[0]
    total = jnp.sum(win[...].astype(F32), axis=0)
    wsum[...] = total[:share].astype(BF16)
    bout[...] = total[share:]

    def publish(k, carry):
        remote(wsum, wout.at[me], vs, vr, place(lax.rem(me + k, N))).start()
        return carry

    ownx.wait()
    for m in range(1, R):
        at = Zp.at[lax.rem(r - m + R, R)]
        pltpu.make_async_copy(at, at, xr.at[m]).wait()
    zcps = []
    for k in range(1, C):
        to = lax.rem(c + k, C)
        src = Zp.at[to // ratio, rows(lax.rem(to, ratio) * NI, NI)]
        cp = remote(src, zin.at[k - 1], zs.at[k], zr.at[k], (r, to, d))
        cp.start()
        zcps.append(cp)
    started += zcps
    lax.fori_loop(1, N, publish, 0)
    ownv = pltpu.make_async_copy(wsum, wout.at[me], ls.at[3])
    ownv.start()
    total = Zp[c // ratio, rows(lax.rem(c, ratio) * NI, NI), :].astype(F32)
    for k in range(1, C):
        zcps[k - 1].wait_recv()
        total = total + zin[k - 1].astype(F32)
    fin[...] = total.astype(BF16)
    here = glout.at[:, lanes(r * H, H)]
    ownf = pltpu.make_async_copy(fin, here, ls.at[4])
    ownf.start()
    for m in range(1, R):
        cp = remote(fin, here, fs.at[m], fr.at[m], (lax.rem(r + m, R), c, d))
        cp.start()
        started.append(cp)
    owng.wait()
    for k in range(1, RD):
        at = grin.at[lax.rem(slot - k + RD, RD)]
        pltpu.make_async_copy(at, at, grr.at[k]).wait()
    for q in range(D):
        total = grin[q].astype(F32)
        for h in range(1, R):
            total = total + grin[h * D + q].astype(F32)
        grout[q] = total.astype(BF16)
    ownf.wait()
    for m in range(1, R):
        at = glout.at[:, lanes(lax.rem(r - m + R, R) * H, H)]
        pltpu.make_async_copy(at, at, fr.at[m]).wait()
    ownv.wait()
    most = wout.at[pl.ds(0, N - 1)]
    pltpu.make_async_copy(most, most, vr).wait()
    pltpu.make_async_copy(most, most, vs).wait()
    pltpu.make_async_copy(win.at[pl.ds(0, N - 1)], win.at[pl.ds(0, N - 1)], ws).wait()
    for cp in started:
        cp.wait_send()


VM = pl.BlockSpec(memory_space=pltpu.VMEM)


def body(alignment_matrix, twin_linear_matrix, final_matrix, final_offset, adjoint_incoming):
    SL, NI, _ = alignment_matrix.shape
    CH = twin_linear_matrix.shape[1] // 2
    O = final_matrix.shape[1]
    R, C, D = lax.axis_size("row"), lax.axis_size("col"), lax.axis_size("depth")
    N = R * C * D
    S = SL * D
    crop = NI * C
    block_i, J, _ = adjoint_incoming.shape
    ratio = C // R
    W = CH * SL
    H = W // R
    DMA = pltpu.SemaphoreType.DMA
    standardized, backprop = jax.vjp(standardize_channels, alignment_matrix.astype(F32))
    normed = standardized.astype(BF16)
    panels = jnp.dot(normed, twin_linear_matrix, preferred_element_type=F32).astype(BF16)
    lt = jnp.transpose(panels[..., :CH], (1, 2, 0)).reshape(NI, W)
    rt = jnp.transpose(panels[..., CH:].reshape(SL, D, J, CH), (1, 3, 2, 0)).reshape(D, CH, J * SL)
    L, rall = pl.pallas_call(
        functools.partial(gather_kernel, R, C, D),
        out_shape=(
            jax.ShapeDtypeStruct((block_i, D * W), BF16),
            jax.ShapeDtypeStruct((D, CH, J * SL), BF16),
        ),
        in_specs=[VM] * 2,
        out_specs=(VM, VM),
        scratch_shapes=[
            pltpu.VMEM((C, NI, H), BF16),
            DMA((C,)), DMA((C,)), DMA((R, ratio)), DMA((R, ratio)),
            DMA((D, R, ratio)), DMA((D, R, ratio)), DMA((D,)), DMA((D,)), DMA((ratio,)),
        ],
        compiler_params=pltpu.CompilerParams(collective_id=0, has_side_effects=True),
        name="gather_panels",
    )(lt, rt)
    RT = jnp.transpose(rall.reshape(D, CH, J, SL), (1, 2, 0, 3)).reshape(CH, J * S)
    RM = RT.T
    WF = jnp.transpose(final_matrix.reshape(CH, CH, O), (1, 0, 2)).reshape(CH, CH * O)
    WR = WF.T
    A = adjoint_incoming.reshape(block_i, J * O)
    JB = 4 if J % 4 == 0 else 1
    pair, gl, gr, w, bsum = pl.pallas_call(
        functools.partial(pair_kernel, D, SL, CH, JB, S, crop),
        grid=(J // JB,),
        out_shape=(
            jax.ShapeDtypeStruct((block_i, J * O), BF16),
            jax.ShapeDtypeStruct((block_i, D * W), BF16),
            jax.ShapeDtypeStruct((J * S, CH), F32),
            jax.ShapeDtypeStruct((CH, CH * O), F32),
            jax.ShapeDtypeStruct((8, O), F32),
        ),
        in_specs=[
            VM,
            pl.BlockSpec((block_i, JB * O), lambda g: (0, g)),
            pl.BlockSpec((JB * S, CH), lambda g: (g, 0)),
            pl.BlockSpec((CH, JB * S), lambda g: (0, g)),
            VM, VM, VM,
        ],
        out_specs=(
            pl.BlockSpec((block_i, JB * O), lambda g: (0, g)),
            VM,
            pl.BlockSpec((JB * S, CH), lambda g: (g, 0)),
            VM, VM,
        ),
        scratch_shapes=[
            pltpu.VMEM((D * W, block_i), BF16),
            pltpu.VMEM((D * W, JB * O), BF16),
            pltpu.VMEM((JB * S, CH * O), BF16),
            pltpu.VMEM((block_i, D * W), F32),
            pltpu.VMEM((CH, CH * O), F32),
            pltpu.VMEM((8, O), F32),
        ],
        compiler_params=pltpu.CompilerParams(vmem_limit_bytes=60 * 1024 * 1024),
        name="pair_products",
    )(L, A, RM, RT, WF, WR, final_offset.reshape(1, O))
    contact_delta = pair.reshape(block_i, J, O)
    grt = jnp.transpose(gr.astype(BF16).reshape(J, D, SL, CH), (1, 3, 0, 2)).reshape(D, CH, J * SL)
    share = CH * CH // N
    pad = 16
    wrows = jnp.transpose(w.reshape(CH, CH, O), (1, 0, 2)).astype(BF16).reshape(N, share, O)
    brow = jnp.pad(bsum[0:1].astype(BF16), ((0, pad - 1), (0, 0)))
    wv = jnp.concatenate([wrows, jnp.broadcast_to(brow[None], (N, pad, O))], axis=1)
    glout, grout, wout, bout = pl.pallas_call(
        functools.partial(reduce_kernel, R, C, D),
        out_shape=(
            jax.ShapeDtypeStruct((NI, W), BF16),
            jax.ShapeDtypeStruct((D, CH, J * SL), BF16),
            jax.ShapeDtypeStruct((N, share, O), BF16),
            jax.ShapeDtypeStruct((pad, O), F32),
        ),
        in_specs=[VM] * 3,
        out_specs=(VM,) * 4,
        scratch_shapes=[
            pltpu.VMEM((2, block_i, W), BF16),
            pltpu.VMEM((block_i, W), BF16),
            pltpu.VMEM((block_i, W), BF16),
            pltpu.VMEM((R, block_i, H), BF16),
            pltpu.VMEM((R, block_i, H), BF16),
            pltpu.VMEM((C - 1, NI, H), BF16),
            pltpu.VMEM((NI, H), BF16),
            pltpu.VMEM((R * D, CH, J * SL), BF16),
            pltpu.VMEM((N, share + pad, O), BF16),
            pltpu.VMEM((share, O), BF16),
            DMA((2,)), DMA((2,)), DMA, DMA, DMA((R,)), DMA((R,)), DMA((C,)), DMA((C,)),
            DMA((R,)), DMA((R,)), DMA((R * D,)), DMA((R * D,)), DMA, DMA, DMA, DMA, DMA((5,)),
        ],
        compiler_params=pltpu.CompilerParams(collective_id=1, has_side_effects=True),
        name="reduce_grads",
    )(gl, grt, wv)
    left = jnp.transpose(glout.reshape(NI, CH, SL), (2, 0, 1))
    right = jnp.transpose(grout.reshape(D, CH, J, SL), (3, 0, 2, 1)).reshape(SL, NI, CH)
    grad_panels = jnp.concatenate([left, right], axis=-1)
    adjoint = jnp.einsum("slk,mk->slm", grad_panels, twin_linear_matrix, preferred_element_type=F32)
    return (
        contact_delta,
        backprop(adjoint)[0],
        wout.reshape(CH * CH, O).astype(F32),
        bout[0],
    )


def solution(mesh):
    in_specs = (P("depth", "col", None), P(), P(), P(), P("row", ("col", "depth"), None))
    out_specs = (P("row", ("col", "depth"), None), P("depth", "col", None), P(), P())
    return jax.shard_map(body, mesh=mesh, in_specs=in_specs, out_specs=out_specs, check_vma=False)
```

```python
import functools

import jax
import jax.numpy as jnp
from jax import lax
from jax.experimental import pallas as pl
from jax.experimental.pallas import tpu as pltpu
from jax.sharding import PartitionSpec as P

epsilon = 1e-05
MESH = pl.DeviceIdType.MESH
F32 = jnp.float32
BF16 = jnp.bfloat16


def standardize_channels(values):
    centre = jnp.mean(values, axis=-1, keepdims=True)
    spread = jnp.mean(jnp.square(values - centre), axis=-1, keepdims=True)
    return (values - centre) * lax.rsqrt(spread + epsilon)


def remote(src, dst, send, recv, where):
    return pltpu.make_async_remote_copy(
        src_ref=src, dst_ref=dst, send_sem=send, recv_sem=recv, device_id=where, device_id_type=MESH
    )


def lanes(start, size):
    return pl.ds(pl.multiple_of(start, 128), size)


def rows(start, size):
    return pl.ds(pl.multiple_of(start, size), size)


def fused_kernel(
    R, C, D, crop,
    lt, rt, A, WF, off,
    pair, glout, grout, wout, bout,
    L, rall, T, U, gl, grT, wacc, Z, cbuf, ysrc, ybuf, xsrc, Zp, zin, fin, grin, wv, win, wsum,
    zs, zr, xs, xr, ps, pr, rs, rr, lsem,
    cs, cr, ys, yr, bxs, bxr, bzs, bzr, fs, fr, gs, grr, ws, wr, vs, vr, ls,
):
    r, c, d = lax.axis_index("row"), lax.axis_index("col"), lax.axis_index("depth")
    N = R * C * D
    me = (r * C + c) * D + d
    NI, W = lt.shape
    H = W // R
    ratio = C // R
    CH, JS = rt.shape[1:]
    O = off.shape[1]
    J = A.shape[1] // O
    SL = JS // J
    S = SL * D
    near = d + 1 - 2 * lax.rem(d, 2)
    far = lax.rem(d + 2, D)
    nearfar = lax.rem(near + 2, D)

    def place(t):
        return (t // (C * D), lax.rem(t // D, C), lax.rem(t, D))

    barrier = pltpu.get_barrier_semaphore()

    def greet(k, carry):
        pl.semaphore_signal(barrier, inc=1, device_id=place(lax.rem(me + k, N)), device_id_type=MESH)
        return carry

    lax.fori_loop(1, N, greet, 0)
    pl.semaphore_wait(barrier, N - 1)
    sends = []

    def launch(cp):
        cp.start()
        sends.append(cp)

    def arrived(at, sem):
        pltpu.make_async_copy(at, at, sem).wait()

    ownr = pltpu.make_async_copy(rt.at[d], rall.at[d], rs.at[0])
    ownr.start()
    for k in range(1, D):
        t = lax.rem(d + k, D)
        launch(remote(rt.at[t], rall.at[d], rs.at[k], rr.at[k], (r, c, t)))
    mine = lt.at[:, lanes(r * H, H)]
    pltpu.make_async_copy(mine, Z.at[c], zr.at[0]).start()
    for k in range(1, C):
        launch(remote(mine, Z.at[c], zs.at[k], zr.at[k], (r, lax.rem(c + k, C), d)))
    total = jnp.sum(A[...].astype(F32), axis=0, keepdims=True)
    bias = total[:, :O]
    for j in range(1, J):
        bias = bias + total[:, j * O : (j + 1) * O]
    bias = bias * (1.0 / crop)

    ownr.wait()
    for k in range(1, D):
        arrived(rall.at[lax.rem(d - k + D, D)], rr.at[k])

    def spot(b, m, who):
        return L.at[who, pl.ds(b * NI, NI), lanes(lax.rem(r - m + R, R) * H, H)]

    def forward_row():
        for m in range(R - 1, -1, -1):
            to = lax.rem(r + m, R)
            for b in range(ratio):
                block = to * ratio + b
                arrived(Z.at[block], zr.at[lax.rem(c - block + C, C)])
                dst = L.at[d, pl.ds(b * NI, NI), lanes(r * H, H)]
                if m:
                    remote(Z.at[block], dst, xs.at[m, b], xr.at[m, b], (to, c, d)).start()
                else:
                    local = pltpu.make_async_copy(Z.at[block], dst, lsem.at[b])
                    local.start()
                    local.wait()
                    spread_depth(b, 0)

    def spread_depth(b, m):
        at = spot(b, m, d)
        remote(at, at, ps.at[1, m, b], pr.at[1, m, b], (r, c, far)).start()
        remote(at, at, ps.at[0, m, b], pr.at[0, m, b], (r, c, near)).start()

    def forward_depth():
        for m in range(1, R):
            for b in range(ratio):
                arrived(spot(b, m, d), xr.at[m, b])
                spread_depth(b, m)

    def forward_core():
        for m in range(R):
            for b in range(ratio):
                at = spot(b, m, far)
                arrived(at, pr.at[1, m, b])
                remote(at, at, ps.at[2, m, b], pr.at[2, m, b], (r, c, near)).start()

    def finish_gather():
        for m in range(R):
            for b in range(ratio):
                arrived(spot(b, m, near), pr.at[0, m, b])
                arrived(spot(b, m, nearfar), pr.at[2, m, b])

    def settle_gather():
        for m in range(R):
            for b in range(ratio):
                if m:
                    at = spot(b, m, d)
                    pltpu.make_async_copy(at, at, xs.at[m, b]).wait()
                for slot in range(3):
                    at = spot(b, m, d)
                    pltpu.make_async_copy(at, at, ps.at[slot, m, b]).wait()

    first = remote(gl.at[nearfar], cbuf.at[1], cs.at[1], cr.at[1], (r, c, near))
    second = remote(gl.at[near], cbuf.at[0], cs.at[0], cr.at[0], (r, c, near))
    ycp = remote(ysrc, ybuf, ys, yr, (r, c, far))

    def order(i):
        base = jnp.where(i < 2, near, d)
        return lax.rem(base + 2 * lax.rem(i + 1, 2), D)

    part = min(1024, CH * O)

    def left_grad(i, carry):
        g = order(i)
        right = rall[g].T
        for n in range(CH * O // part):
            made = jnp.dot(right, WF[:, n * part : (n + 1) * part], preferred_element_type=F32).astype(BF16)
            for q in range(part // O):
                k = n * (part // O) + q
                for j in range(J):
                    T[g, k * SL : (k + 1) * SL, j * O : (j + 1) * O] = made[
                        j * SL : (j + 1) * SL, q * O : (q + 1) * O
                    ]
        gl[g] = (
            lax.dot_general(A[...], T[g], (((1,), (1,)), ((), ())), preferred_element_type=F32) * (1.0 / S)
        ).astype(BF16)

        @pl.when(i == 0)
        def _():
            first.start()

        @pl.when(i == 1)
        def _():
            second.start()
            forward_row()

        @pl.when(i == 2)
        def _():
            first.wait_recv()
            ysrc[...] = (gl[far].astype(F32) + cbuf[1].astype(F32)).astype(BF16)
            forward_depth()
            ycp.start()

        @pl.when(i == 3)
        def _():
            forward_core()

        return carry

    lax.fori_loop(0, D, left_grad, 0)
    second.wait_recv()
    finish_gather()

    wide = 4 * O if J % 4 == 0 else O
    offset = jnp.concatenate([off[...]] * (wide // O), axis=1)

    def pair_block(n, carry):
        cut = lanes(n * wide, wide)
        made = jnp.dot(L[0], T[0, :, cut], preferred_element_type=F32)
        for g in range(1, D):
            made = made + jnp.dot(L[g], T[g, :, cut], preferred_element_type=F32)
        pair[:, cut] = (made * (1.0 / S) + offset).astype(BF16)
        return carry

    lax.fori_loop(0, J * O // wide, pair_block, 0)

    ycp.wait_recv()
    for h in range(R):
        cut = slice(h * H, (h + 1) * H)
        xsrc[h] = (
            gl[d, :, cut].astype(F32) + cbuf[0, :, cut].astype(F32) + ybuf[:, cut].astype(F32)
        ).astype(BF16)
    ownx = pltpu.make_async_copy(xsrc.at[r], Zp.at[r], ls.at[2])
    ownx.start()
    for m in range(1, R):
        to = lax.rem(r + m, R)
        launch(remote(xsrc.at[to], Zp.at[r], bxs.at[m], bxr.at[m], (to, c, d)))
    ownx.wait()

    RD = R * D
    slot = r * D + d
    zcps = []
    for k in range(1, C):
        to = lax.rem(c + k, C)
        src = Zp.at[to // ratio, rows(lax.rem(to, ratio) * NI, NI)]
        zcps.append(remote(src, zin.at[k - 1], bzs.at[k], bzr.at[k], (r, to, d)))
    fcps = []
    here = glout.at[:, lanes(r * H, H)]
    for m in range(1, R):
        fcps.append(remote(fin, here, fs.at[m], fr.at[m], (lax.rem(r + m, R), c, d)))
    ownf = pltpu.make_async_copy(fin, here, ls.at[4])
    sends.extend(zcps)
    sends.extend(fcps)
    wacc[...] = jnp.zeros_like(wacc)
    quarter = W // 4

    def right_grad(i, carry):
        g = order(i)
        for n in range(4):
            made = lax.dot_general(
                L[g, :, n * quarter : (n + 1) * quarter], A[...], (((0,), (0,)), ((), ())),
                preferred_element_type=F32,
            ).astype(BF16)
            for q in range(quarter // SL):
                k = n * (quarter // SL) + q
                for j in range(J):
                    U[j * SL : (j + 1) * SL, k * O : (k + 1) * O] = made[
                        q * SL : (q + 1) * SL, j * O : (j + 1) * O
                    ]
        grT[g] = (
            lax.dot_general(WF[...], U[...], (((1,), (1,)), ((), ())), preferred_element_type=F32) * (1.0 / S)
        ).astype(BF16)
        wacc[...] += jnp.dot(rall[g], U[...], preferred_element_type=F32)

        @pl.when(i == 0)
        def _():
            for m in range(1, R):
                arrived(Zp.at[lax.rem(r - m + R, R)], bxr.at[m])
            for cp in zcps:
                cp.start()

        @pl.when(i == 2)
        def _():
            total = Zp[c // ratio, rows(lax.rem(c, ratio) * NI, NI), :].astype(F32)
            for k in range(1, C):
                zcps[k - 1].wait_recv()
                total = total + zin[k - 1].astype(F32)
            fin[...] = total.astype(BF16)
            ownf.start()
            for cp in fcps:
                cp.start()

        return carry

    lax.fori_loop(0, D, right_grad, 0)

    share, pad = wsum.shape[0], bout.shape[0]
    cuts = CH // share
    scale = 1.0 / (S * crop)
    row = jnp.broadcast_to(bias, (pad, O)).astype(BF16)
    for k in range(CH):
        for p in range(cuts):
            wv[k * cuts + p, 0:share] = (
                wacc[p * share : (p + 1) * share, k * O : (k + 1) * O] * scale
            ).astype(BF16)
            wv[k * cuts + p, share : share + pad] = row

    def spread(k, carry):
        t = lax.rem(me + k, N)
        remote(wv.at[t], win.at[me], ws, wr, place(t)).start()
        return carry

    lax.fori_loop(1, N, spread, 0)
    ownw = pltpu.make_async_copy(wv.at[me], win.at[me], ls.at[0])
    ownw.start()
    for k in range(1, RD):
        t = lax.rem(slot + k, RD)
        launch(
            remote(grT.at[lax.rem(t, D)], grin.at[slot], gs.at[k], grr.at[k], (t // D, c, lax.rem(t, D)))
        )
    owng = pltpu.make_async_copy(grT.at[d], grin.at[slot], ls.at[1])
    owng.start()
    ownw.wait()
    most = win.at[pl.ds(0, N - 1)]
    arrived(most, wr)
    total = win[0].astype(F32)
    for k in range(1, N):
        total = total + win[k].astype(F32)
    wsum[...] = total[:share].astype(BF16)
    bout[...] = total[share:]

    def publish(k, carry):
        remote(wsum, wout.at[me], vs, vr, place(lax.rem(me + k, N))).start()
        return carry

    lax.fori_loop(1, N, publish, 0)
    ownv = pltpu.make_async_copy(wsum, wout.at[me], ls.at[3])
    ownv.start()
    owng.wait()
    for k in range(1, RD):
        arrived(grin.at[lax.rem(slot - k + RD, RD)], grr.at[k])
    for q in range(D):
        total = grin[q].astype(F32)
        for h in range(1, R):
            total = total + grin[h * D + q].astype(F32)
        grout[q] = total.astype(BF16)
    ownf.wait()
    for m in range(1, R):
        arrived(glout.at[:, lanes(lax.rem(r - m + R, R) * H, H)], fr.at[m])
    settle_gather()
    first.wait_send()
    second.wait_send()
    ycp.wait_send()
    for cp in sends:
        cp.wait_send()
    arrived(most, ws)
    ownv.wait()
    most = wout.at[pl.ds(0, N - 1)]
    arrived(most, vr)
    arrived(most, vs)


VM = pl.BlockSpec(memory_space=pltpu.VMEM)


def body(alignment_matrix, twin_linear_matrix, final_matrix, final_offset, adjoint_incoming):
    SL, NI, _ = alignment_matrix.shape
    CH = twin_linear_matrix.shape[1] // 2
    O = final_matrix.shape[1]
    R, C, D = lax.axis_size("row"), lax.axis_size("col"), lax.axis_size("depth")
    N = R * C * D
    S = SL * D
    crop = NI * C
    block_i, J, _ = adjoint_incoming.shape
    ratio = C // R
    W = CH * SL
    H = W // R
    DMA = pltpu.SemaphoreType.DMA
    standardized, backprop = jax.vjp(standardize_channels, alignment_matrix.astype(F32))
    normed = standardized.astype(BF16)
    panels = jnp.dot(normed, twin_linear_matrix, preferred_element_type=F32).astype(BF16)
    lt = jnp.transpose(panels[..., :CH], (1, 2, 0)).reshape(NI, W)
    rt = jnp.transpose(panels[..., CH:].reshape(SL, D, J, CH), (1, 3, 2, 0)).reshape(D, CH, J * SL)
    WF = jnp.transpose(final_matrix.reshape(CH, CH, O), (1, 0, 2)).reshape(CH, CH * O)
    A = adjoint_incoming.reshape(block_i, J * O)
    share = CH * CH // N
    pad = 16
    JS = J * SL

    def vb(*shape):
        return pltpu.VMEM(shape, BF16)

    pair, glout, grout, wout, bout = pl.pallas_call(
        functools.partial(fused_kernel, R, C, D, crop),
        out_shape=(
            jax.ShapeDtypeStruct((block_i, J * O), BF16),
            jax.ShapeDtypeStruct((NI, W), BF16),
            jax.ShapeDtypeStruct((D, CH, JS), BF16),
            jax.ShapeDtypeStruct((N, share, O), BF16),
            jax.ShapeDtypeStruct((pad, O), F32),
        ),
        in_specs=[VM] * 5,
        out_specs=(VM,) * 5,
        scratch_shapes=[
            vb(D, block_i, W), vb(D, CH, JS), vb(D, W, J * O), vb(JS, CH * O), vb(D, block_i, W),
            vb(D, CH, JS), pltpu.VMEM((CH, CH * O), F32), vb(C, NI, H), vb(2, block_i, W),
            vb(block_i, W), vb(block_i, W), vb(R, block_i, H), vb(R, block_i, H), vb(C - 1, NI, H),
            vb(NI, H), vb(R * D, CH, JS), vb(N, share + pad, O), vb(N, share + pad, O), vb(share, O),
            DMA((C,)), DMA((C,)), DMA((R, ratio)), DMA((R, ratio)),
            DMA((3, R, ratio)), DMA((3, R, ratio)), DMA((D,)), DMA((D,)), DMA((ratio,)),
            DMA((2,)), DMA((2,)), DMA, DMA, DMA((R,)), DMA((R,)), DMA((C,)), DMA((C,)),
            DMA((R,)), DMA((R,)), DMA((R * D,)), DMA((R * D,)), DMA, DMA, DMA, DMA, DMA((5,)),
        ],
        compiler_params=pltpu.CompilerParams(
            collective_id=0, has_side_effects=True, vmem_limit_bytes=63 * 1024 * 1024
        ),
        name="pair_and_exchange",
    )(lt, rt, A, WF, final_offset.reshape(1, O))
    contact_delta = pair.reshape(block_i, J, O)
    left = jnp.transpose(glout.reshape(NI, CH, SL), (2, 0, 1))
    right = jnp.transpose(grout.reshape(D, CH, J, SL), (3, 0, 2, 1)).reshape(SL, NI, CH)
    grad_panels = jnp.concatenate([left, right], axis=-1)
    adjoint = jnp.einsum("slk,mk->slm", grad_panels, twin_linear_matrix, preferred_element_type=F32)
    return (
        contact_delta,
        backprop(adjoint)[0],
        wout.reshape(CH * CH, O).astype(F32),
        bout[0],
    )


def solution(mesh):
    in_specs = (P("depth", "col", None), P(), P(), P(), P("row", ("col", "depth"), None))
    out_specs = (P("row", ("col", "depth"), None), P("depth", "col", None), P(), P())
    return jax.shard_map(body, mesh=mesh, in_specs=in_specs, out_specs=out_specs, check_vma=False)
```

```python
import functools

import jax
import jax.numpy as jnp
from jax import lax
from jax.experimental import pallas as pl
from jax.experimental.pallas import tpu as pltpu
from jax.sharding import PartitionSpec as P

epsilon = 1e-05
MESH = pl.DeviceIdType.MESH
F32 = jnp.float32
BF16 = jnp.bfloat16


def standardize_channels(values):
    centre = jnp.mean(values, axis=-1, keepdims=True)
    spread = jnp.mean(jnp.square(values - centre), axis=-1, keepdims=True)
    return (values - centre) * lax.rsqrt(spread + epsilon)


def remote(src, dst, send, recv, where):
    return pltpu.make_async_remote_copy(
        src_ref=src, dst_ref=dst, send_sem=send, recv_sem=recv, device_id=where, device_id_type=MESH
    )


def lanes(start, size):
    return pl.ds(pl.multiple_of(start, 128), size)


def rows(start, size):
    return pl.ds(pl.multiple_of(start, size), size)


def fused_kernel(
    R, C, D, crop,
    lt, rt, A, WF, off,
    pair, glout, grout, wout, bout,
    L, rall, T, U, gl, grT, wacc, Z, cbuf, ysrc, ybuf, xsrc, Zp, zin, fin, grin, wv, win, wsum,
    zs, zr, xs, xr, ps, pr, rs, rr, lsem,
    cs, cr, ys, yr, bxs, bxr, bzs, bzr, fs, fr, gs, grr, ws, wr, vs, vr, ls,
):
    r, c, d = lax.axis_index("row"), lax.axis_index("col"), lax.axis_index("depth")
    N = R * C * D
    me = (r * C + c) * D + d
    NI, W = lt.shape
    H = W // R
    ratio = C // R
    CH, JS = rt.shape[1:]
    O = off.shape[1]
    J = A.shape[1] // O
    SL = JS // J
    S = SL * D
    near = d + 1 - 2 * lax.rem(d, 2)
    far = lax.rem(d + 2, D)
    nearfar = lax.rem(near + 2, D)

    def place(t):
        return (t // (C * D), lax.rem(t // D, C), lax.rem(t, D))

    barrier = pltpu.get_barrier_semaphore()

    def greet(k, carry):
        pl.semaphore_signal(barrier, inc=1, device_id=place(lax.rem(me + k, N)), device_id_type=MESH)
        return carry

    lax.fori_loop(1, N, greet, 0)
    pl.semaphore_wait(barrier, N - 1)
    sends = []

    def launch(cp):
        cp.start()
        sends.append(cp)

    def arrived(at, sem):
        pltpu.make_async_copy(at, at, sem).wait()

    ownr = pltpu.make_async_copy(rt.at[d], rall.at[d], rs.at[0])
    ownr.start()
    for k in range(1, D):
        t = lax.rem(d + k, D)
        launch(remote(rt.at[t], rall.at[d], rs.at[k], rr.at[k], (r, c, t)))
    mine = lt.at[:, lanes(r * H, H)]
    pltpu.make_async_copy(mine, Z.at[c], zr.at[0]).start()
    for k in range(1, C):
        launch(remote(mine, Z.at[c], zs.at[k], zr.at[k], (r, lax.rem(c + k, C), d)))
    total = jnp.sum(A[...].astype(F32), axis=0, keepdims=True)
    bias = total[:, :O]
    for j in range(1, J):
        bias = bias + total[:, j * O : (j + 1) * O]
    bias = bias * (1.0 / crop)

    ownr.wait()
    for k in range(1, D):
        arrived(rall.at[lax.rem(d - k + D, D)], rr.at[k])

    def spot(b, m, who):
        return L.at[who, pl.ds(b * NI, NI), lanes(lax.rem(r - m + R, R) * H, H)]

    def forward_row():
        for m in range(R - 1, -1, -1):
            to = lax.rem(r + m, R)
            for b in range(ratio):
                block = to * ratio + b
                arrived(Z.at[block], zr.at[lax.rem(c - block + C, C)])
                dst = L.at[d, pl.ds(b * NI, NI), lanes(r * H, H)]
                if m:
                    remote(Z.at[block], dst, xs.at[m, b], xr.at[m, b], (to, c, d)).start()
                else:
                    local = pltpu.make_async_copy(Z.at[block], dst, lsem.at[b])
                    local.start()
                    local.wait()
                    spread_depth(b, 0)

    def spread_depth(b, m):
        at = spot(b, m, d)
        remote(at, at, ps.at[1, m, b], pr.at[1, m, b], (r, c, far)).start()
        remote(at, at, ps.at[0, m, b], pr.at[0, m, b], (r, c, near)).start()

    def forward_depth():
        for m in range(1, R):
            for b in range(ratio):
                arrived(spot(b, m, d), xr.at[m, b])
                spread_depth(b, m)

    def forward_core():
        for m in range(R):
            for b in range(ratio):
                at = spot(b, m, far)
                arrived(at, pr.at[1, m, b])
                remote(at, at, ps.at[2, m, b], pr.at[2, m, b], (r, c, near)).start()

    def finish_gather(who, slot):
        for m in range(R):
            for b in range(ratio):
                arrived(spot(b, m, who), pr.at[slot, m, b])

    def settle_gather():
        for m in range(R):
            for b in range(ratio):
                if m:
                    at = spot(b, m, d)
                    pltpu.make_async_copy(at, at, xs.at[m, b]).wait()
                for slot in range(3):
                    at = spot(b, m, d)
                    pltpu.make_async_copy(at, at, ps.at[slot, m, b]).wait()

    first = remote(gl.at[nearfar], cbuf.at[1], cs.at[1], cr.at[1], (r, c, near))
    second = remote(gl.at[near], cbuf.at[0], cs.at[0], cr.at[0], (r, c, near))
    ycp = remote(ysrc, ybuf, ys, yr, (r, c, far))

    def order(i):
        base = jnp.where(i < 2, near, d)
        return lax.rem(base + 2 * lax.rem(i + 1, 2), D)

    part = min(1024, CH * O)

    def left_grad(i, carry):
        g = order(i)
        right = rall[g].T
        for n in range(CH * O // part):
            made = jnp.dot(right, WF[:, n * part : (n + 1) * part], preferred_element_type=F32).astype(BF16)
            for q in range(part // O):
                k = n * (part // O) + q
                for j in range(J):
                    T[g, k * SL : (k + 1) * SL, j * O : (j + 1) * O] = made[
                        j * SL : (j + 1) * SL, q * O : (q + 1) * O
                    ]
        gl[g] = (
            lax.dot_general(A[...], T[g], (((1,), (1,)), ((), ())), preferred_element_type=F32) * (1.0 / S)
        ).astype(BF16)

        @pl.when(i == 0)
        def _():
            first.start()

        @pl.when(i == 1)
        def _():
            second.start()
            forward_row()

        @pl.when(i == 2)
        def _():
            first.wait_recv()
            ysrc[...] = (gl[far].astype(F32) + cbuf[1].astype(F32)).astype(BF16)
            forward_depth()
            ycp.start()

        return carry

    lax.fori_loop(0, D, left_grad, 0)

    ownx = pltpu.make_async_copy(xsrc.at[r], Zp.at[r], ls.at[2])
    xcps = []
    for m in range(1, R):
        to = lax.rem(r + m, R)
        xcps.append(remote(xsrc.at[to], Zp.at[r], bxs.at[m], bxr.at[m], (to, c, d)))
    sends.extend(xcps)

    RD = R * D
    slot = r * D + d
    zcps = []
    for k in range(1, C):
        to = lax.rem(c + k, C)
        src = Zp.at[to // ratio, rows(lax.rem(to, ratio) * NI, NI)]
        zcps.append(remote(src, zin.at[k - 1], bzs.at[k], bzr.at[k], (r, to, d)))
    fcps = []
    here = glout.at[:, lanes(r * H, H)]
    for m in range(1, R):
        fcps.append(remote(fin, here, fs.at[m], fr.at[m], (lax.rem(r + m, R), c, d)))
    ownf = pltpu.make_async_copy(fin, here, ls.at[4])
    sends.extend(zcps)
    sends.extend(fcps)
    wacc[...] = jnp.zeros_like(wacc)
    quarter = W // 4

    def right_grad(i, carry):
        g = lax.rem(jnp.where(i < 2, d, near) + 2 * lax.rem(i, 2), D)
        for n in range(4):
            made = lax.dot_general(
                L[g, :, n * quarter : (n + 1) * quarter], A[...], (((0,), (0,)), ((), ())),
                preferred_element_type=F32,
            ).astype(BF16)
            for q in range(quarter // SL):
                k = n * (quarter // SL) + q
                for j in range(J):
                    U[j * SL : (j + 1) * SL, k * O : (k + 1) * O] = made[
                        q * SL : (q + 1) * SL, j * O : (j + 1) * O
                    ]
        grT[g] = (
            lax.dot_general(WF[...], U[...], (((1,), (1,)), ((), ())), preferred_element_type=F32) * (1.0 / S)
        ).astype(BF16)
        wacc[...] += jnp.dot(rall[g], U[...], preferred_element_type=F32)

        @pl.when(i == 0)
        def _():
            forward_core()
            second.wait_recv()
            ycp.wait_recv()
            for h in range(R):
                cut = slice(h * H, (h + 1) * H)
                xsrc[h] = (
                    gl[d, :, cut].astype(F32) + cbuf[0, :, cut].astype(F32) + ybuf[:, cut].astype(F32)
                ).astype(BF16)
            ownx.start()
            for cp in xcps:
                cp.start()

        @pl.when(i == 1)
        def _():
            finish_gather(near, 0)
            ownx.wait()
            for m in range(1, R):
                arrived(Zp.at[lax.rem(r - m + R, R)], bxr.at[m])
            for cp in zcps:
                cp.start()

        @pl.when(i == 2)
        def _():
            finish_gather(nearfar, 2)

        @pl.when(i == 3)
        def _():
            total = Zp[c // ratio, rows(lax.rem(c, ratio) * NI, NI), :].astype(F32)
            for k in range(1, C):
                zcps[k - 1].wait_recv()
                total = total + zin[k - 1].astype(F32)
            fin[...] = total.astype(BF16)
            ownf.start()
            for cp in fcps:
                cp.start()

        return carry

    lax.fori_loop(0, D, right_grad, 0)

    share, pad = wsum.shape[0], bout.shape[0]
    cuts = CH // share
    scale = 1.0 / (S * crop)
    row = jnp.broadcast_to(bias, (pad, O)).astype(BF16)
    for k in range(CH):
        for p in range(cuts):
            wv[k * cuts + p, 0:share] = (
                wacc[p * share : (p + 1) * share, k * O : (k + 1) * O] * scale
            ).astype(BF16)
            wv[k * cuts + p, share : share + pad] = row

    def spread(k, carry):
        t = lax.rem(me + k, N)
        remote(wv.at[t], win.at[me], ws, wr, place(t)).start()
        return carry

    lax.fori_loop(1, N, spread, 0)
    ownw = pltpu.make_async_copy(wv.at[me], win.at[me], ls.at[0])
    ownw.start()
    for k in range(1, RD):
        t = lax.rem(slot + k, RD)
        launch(
            remote(grT.at[lax.rem(t, D)], grin.at[slot], gs.at[k], grr.at[k], (t // D, c, lax.rem(t, D)))
        )
    owng = pltpu.make_async_copy(grT.at[d], grin.at[slot], ls.at[1])
    owng.start()
    most = win.at[pl.ds(0, N - 1)]
    ownv = pltpu.make_async_copy(wsum, wout.at[me], ls.at[3])

    def publish(k, carry):
        remote(wsum, wout.at[me], vs, vr, place(lax.rem(me + k, N))).start()
        return carry

    def sum_weights():
        ownw.wait()
        arrived(most, wr)
        total = win[0].astype(F32)
        for k in range(1, N):
            total = total + win[k].astype(F32)
        wsum[...] = total[:share].astype(BF16)
        bout[...] = total[share:]
        lax.fori_loop(1, N, publish, 0)
        ownv.start()

    wide = 4 * O if J % 4 == 0 else O
    offset = jnp.concatenate([off[...]] * (wide // O), axis=1)

    half = (J * O // wide) // 2

    def pair_block(n, carry):
        cut = lanes(n * wide, wide)
        made = jnp.dot(L[0], T[0, :, cut], preferred_element_type=F32)
        for g in range(1, D):
            made = made + jnp.dot(L[g], T[g, :, cut], preferred_element_type=F32)
        pair[:, cut] = (made * (1.0 / S) + offset).astype(BF16)
        pl.when(n == half)(sum_weights)
        return carry

    lax.fori_loop(0, J * O // wide, pair_block, 0)

    owng.wait()
    for k in range(1, RD):
        arrived(grin.at[lax.rem(slot - k + RD, RD)], grr.at[k])
    for q in range(D):
        total = grin[q].astype(F32)
        for h in range(1, R):
            total = total + grin[h * D + q].astype(F32)
        grout[q] = total.astype(BF16)
    ownf.wait()
    for m in range(1, R):
        arrived(glout.at[:, lanes(lax.rem(r - m + R, R) * H, H)], fr.at[m])
    settle_gather()
    first.wait_send()
    second.wait_send()
    ycp.wait_send()
    for cp in sends:
        cp.wait_send()
    arrived(most, ws)
    ownv.wait()
    most = wout.at[pl.ds(0, N - 1)]
    arrived(most, vr)
    arrived(most, vs)


VM = pl.BlockSpec(memory_space=pltpu.VMEM)


def body(alignment_matrix, twin_linear_matrix, final_matrix, final_offset, adjoint_incoming):
    SL, NI, _ = alignment_matrix.shape
    CH = twin_linear_matrix.shape[1] // 2
    O = final_matrix.shape[1]
    R, C, D = lax.axis_size("row"), lax.axis_size("col"), lax.axis_size("depth")
    N = R * C * D
    S = SL * D
    crop = NI * C
    block_i, J, _ = adjoint_incoming.shape
    ratio = C // R
    W = CH * SL
    H = W // R
    DMA = pltpu.SemaphoreType.DMA
    standardized, backprop = jax.vjp(standardize_channels, alignment_matrix.astype(F32))
    normed = standardized.astype(BF16)
    panels = jnp.dot(normed, twin_linear_matrix, preferred_element_type=F32).astype(BF16)
    lt = jnp.transpose(panels[..., :CH], (1, 2, 0)).reshape(NI, W)
    rt = jnp.transpose(panels[..., CH:].reshape(SL, D, J, CH), (1, 3, 2, 0)).reshape(D, CH, J * SL)
    WF = jnp.transpose(final_matrix.reshape(CH, CH, O), (1, 0, 2)).reshape(CH, CH * O)
    A = adjoint_incoming.reshape(block_i, J * O)
    share = CH * CH // N
    pad = 16
    JS = J * SL

    def vb(*shape):
        return pltpu.VMEM(shape, BF16)

    pair, glout, grout, wout, bout = pl.pallas_call(
        functools.partial(fused_kernel, R, C, D, crop),
        out_shape=(
            jax.ShapeDtypeStruct((block_i, J * O), BF16),
            jax.ShapeDtypeStruct((NI, W), BF16),
            jax.ShapeDtypeStruct((D, CH, JS), BF16),
            jax.ShapeDtypeStruct((N, share, O), BF16),
            jax.ShapeDtypeStruct((pad, O), F32),
        ),
        in_specs=[VM] * 5,
        out_specs=(VM,) * 5,
        scratch_shapes=[
            vb(D, block_i, W), vb(D, CH, JS), vb(D, W, J * O), vb(JS, CH * O), vb(D, block_i, W),
            vb(D, CH, JS), pltpu.VMEM((CH, CH * O), F32), vb(C, NI, H), vb(2, block_i, W),
            vb(block_i, W), vb(block_i, W), vb(R, block_i, H), vb(R, block_i, H), vb(C - 1, NI, H),
            vb(NI, H), vb(R * D, CH, JS), vb(N, share + pad, O), vb(N, share + pad, O), vb(share, O),
            DMA((C,)), DMA((C,)), DMA((R, ratio)), DMA((R, ratio)),
            DMA((3, R, ratio)), DMA((3, R, ratio)), DMA((D,)), DMA((D,)), DMA((ratio,)),
            DMA((2,)), DMA((2,)), DMA, DMA, DMA((R,)), DMA((R,)), DMA((C,)), DMA((C,)),
            DMA((R,)), DMA((R,)), DMA((R * D,)), DMA((R * D,)), DMA, DMA, DMA, DMA, DMA((5,)),
        ],
        compiler_params=pltpu.CompilerParams(
            collective_id=0, has_side_effects=True, vmem_limit_bytes=63 * 1024 * 1024
        ),
        name="pair_and_exchange",
    )(lt, rt, A, WF, final_offset.reshape(1, O))
    contact_delta = pair.reshape(block_i, J, O)
    left = jnp.transpose(glout.reshape(NI, CH, SL), (2, 0, 1))
    right = jnp.transpose(grout.reshape(D, CH, J, SL), (3, 0, 2, 1)).reshape(SL, NI, CH)
    grad_panels = jnp.concatenate([left, right], axis=-1)
    adjoint = jnp.einsum("slk,mk->slm", grad_panels, twin_linear_matrix, preferred_element_type=F32)
    return (
        contact_delta,
        backprop(adjoint)[0],
        wout.reshape(CH * CH, O).astype(F32),
        bout[0],
    )


def solution(mesh):
    in_specs = (P("depth", "col", None), P(), P(), P(), P("row", ("col", "depth"), None))
    out_specs = (P("row", ("col", "depth"), None), P("depth", "col", None), P(), P())
    return jax.shard_map(body, mesh=mesh, in_specs=in_specs, out_specs=out_specs, check_vma=False)
```

```python
import functools

import jax
import jax.numpy as jnp
from jax import lax
from jax.experimental import pallas as pl
from jax.experimental.pallas import tpu as pltpu
from jax.sharding import PartitionSpec as P

epsilon = 1e-05
MESH = pl.DeviceIdType.MESH
F32 = jnp.float32
BF16 = jnp.bfloat16


def standardize_channels(values):
    centre = jnp.mean(values, axis=-1, keepdims=True)
    spread = jnp.mean(jnp.square(values - centre), axis=-1, keepdims=True)
    return (values - centre) * lax.rsqrt(spread + epsilon)


def remote(src, dst, send, recv, where):
    return pltpu.make_async_remote_copy(
        src_ref=src, dst_ref=dst, send_sem=send, recv_sem=recv, device_id=where, device_id_type=MESH
    )


def lanes(start, size):
    return pl.ds(pl.multiple_of(start, 128), size)


def rows(start, size):
    return pl.ds(pl.multiple_of(start, size), size)


def fused_kernel(
    R, C, D, crop,
    lt, rt, A, WF, off,
    pair, glout, grout, wout, bout,
    L, rall, T, U, gl, grT, wacc, Z, cbuf, ysrc, ybuf, xsrc, Zp, zin, fin, grin, wv, win, wsum,
    zs, zr, xs, xr, ps, pr, rs, rr, lsem,
    cs, cr, ys, yr, bxs, bxr, bzs, bzr, fs, fr, gs, grr, ws, wr, vs, vr, ls,
):
    r, c, d = lax.axis_index("row"), lax.axis_index("col"), lax.axis_index("depth")
    N = R * C * D
    me = (r * C + c) * D + d
    NI, W = lt.shape
    H = W // R
    ratio = C // R
    CH, JS = rt.shape[1:]
    O = off.shape[1]
    J = A.shape[1] // O
    SL = JS // J
    S = SL * D
    near = d + 1 - 2 * lax.rem(d, 2)
    far = lax.rem(d + 2, D)
    nearfar = lax.rem(near + 2, D)

    def place(t):
        return (t // (C * D), lax.rem(t // D, C), lax.rem(t, D))

    barrier = pltpu.get_barrier_semaphore()

    def greet(k, carry):
        pl.semaphore_signal(barrier, inc=1, device_id=place(lax.rem(me + k, N)), device_id_type=MESH)
        return carry

    lax.fori_loop(1, N, greet, 0)
    pl.semaphore_wait(barrier, N - 1)
    sends = []

    def launch(cp):
        cp.start()
        sends.append(cp)

    def arrived(at, sem):
        pltpu.make_async_copy(at, at, sem).wait()

    ownr = pltpu.make_async_copy(rt.at[d], rall.at[d], rs.at[0])
    ownr.start()
    for k in range(1, D):
        t = lax.rem(d + k, D)
        launch(remote(rt.at[t], rall.at[d], rs.at[k], rr.at[k], (r, c, t)))
    mine = lt.at[:, lanes(r * H, H)]
    pltpu.make_async_copy(mine, Z.at[c], zr.at[0]).start()
    for k in range(1, C):
        launch(remote(mine, Z.at[c], zs.at[k], zr.at[k], (r, lax.rem(c + k, C), d)))
    total = jnp.sum(A[...].astype(F32), axis=0, keepdims=True)
    bias = total[:, :O]
    for j in range(1, J):
        bias = bias + total[:, j * O : (j + 1) * O]
    bias = bias * (1.0 / crop)

    ownr.wait()
    for k in range(1, D):
        arrived(rall.at[lax.rem(d - k + D, D)], rr.at[k])

    def spot(b, m, who):
        return L.at[who, pl.ds(b * NI, NI), lanes(lax.rem(r - m + R, R) * H, H)]

    def forward_row():
        for m in range(R - 1, -1, -1):
            to = lax.rem(r + m, R)
            for b in range(ratio):
                block = to * ratio + b
                arrived(Z.at[block], zr.at[lax.rem(c - block + C, C)])
                dst = L.at[d, pl.ds(b * NI, NI), lanes(r * H, H)]
                if m:
                    remote(Z.at[block], dst, xs.at[m, b], xr.at[m, b], (to, c, d)).start()
                else:
                    local = pltpu.make_async_copy(Z.at[block], dst, lsem.at[b])
                    local.start()
                    local.wait()
                    spread_depth(b, 0)

    def spread_depth(b, m):
        at = spot(b, m, d)
        remote(at, at, ps.at[1, m, b], pr.at[1, m, b], (r, c, far)).start()
        remote(at, at, ps.at[0, m, b], pr.at[0, m, b], (r, c, near)).start()

    def forward_depth():
        for m in range(1, R):
            for b in range(ratio):
                arrived(spot(b, m, d), xr.at[m, b])
                spread_depth(b, m)

    def forward_core():
        for m in range(R):
            for b in range(ratio):
                at = spot(b, m, far)
                arrived(at, pr.at[1, m, b])
                remote(at, at, ps.at[2, m, b], pr.at[2, m, b], (r, c, near)).start()

    def finish_gather(who, slot):
        for m in range(R):
            for b in range(ratio):
                arrived(spot(b, m, who), pr.at[slot, m, b])

    def settle_gather():
        for m in range(R):
            for b in range(ratio):
                if m:
                    at = spot(b, m, d)
                    pltpu.make_async_copy(at, at, xs.at[m, b]).wait()
                for slot in range(3):
                    at = spot(b, m, d)
                    pltpu.make_async_copy(at, at, ps.at[slot, m, b]).wait()

    first = remote(gl.at[nearfar], cbuf.at[1], cs.at[1], cr.at[1], (r, c, near))
    second = remote(gl.at[near], cbuf.at[0], cs.at[0], cr.at[0], (r, c, near))
    ycp = remote(ysrc, ybuf, ys, yr, (r, c, far))

    def order(i):
        base = jnp.where(i < 2, near, d)
        return lax.rem(base + 2 * lax.rem(i + 1, 2), D)

    part = min(1024, CH * O)

    def left_grad(i, carry):
        g = order(i)
        right = rall[g].T
        for n in range(CH * O // part):
            made = jnp.dot(right, WF[:, n * part : (n + 1) * part], preferred_element_type=F32).astype(BF16)
            for q in range(part // O):
                k = n * (part // O) + q
                for j in range(J):
                    T[g, k * SL : (k + 1) * SL, j * O : (j + 1) * O] = made[
                        j * SL : (j + 1) * SL, q * O : (q + 1) * O
                    ]
        gl[g] = (
            lax.dot_general(A[...], T[g], (((1,), (1,)), ((), ())), preferred_element_type=F32) * (1.0 / S)
        ).astype(BF16)

        @pl.when(i == 0)
        def _():
            first.start()

        @pl.when(i == 1)
        def _():
            second.start()
            forward_row()

        @pl.when(i == 2)
        def _():
            first.wait_recv()
            ysrc[...] = (gl[far].astype(F32) + cbuf[1].astype(F32)).astype(BF16)
            forward_depth()
            ycp.start()

        return carry

    lax.fori_loop(0, D, left_grad, 0)

    ownx = pltpu.make_async_copy(xsrc.at[r], Zp.at[r], ls.at[2])
    xcps = []
    for m in range(1, R):
        to = lax.rem(r + m, R)
        xcps.append(remote(xsrc.at[to], Zp.at[r], bxs.at[m], bxr.at[m], (to, c, d)))
    sends.extend(xcps)

    RD = R * D
    slot = r * D + d
    zcps = []
    for k in range(1, C):
        to = lax.rem(c + k, C)
        src = Zp.at[to // ratio, rows(lax.rem(to, ratio) * NI, NI)]
        zcps.append(remote(src, zin.at[k - 1], bzs.at[k], bzr.at[k], (r, to, d)))
    fcps = []
    here = glout.at[:, lanes(r * H, H)]
    for m in range(1, R):
        fcps.append(remote(fin, here, fs.at[m], fr.at[m], (lax.rem(r + m, R), c, d)))
    ownf = pltpu.make_async_copy(fin, here, ls.at[4])
    sends.extend(zcps)
    sends.extend(fcps)
    wacc[...] = jnp.zeros_like(wacc)
    quarter = W // 4

    def right_grad(i, carry):
        g = lax.rem(jnp.where(i < 2, d, near) + 2 * lax.rem(i, 2), D)
        for n in range(4):
            made = lax.dot_general(
                L[g, :, n * quarter : (n + 1) * quarter], A[...], (((0,), (0,)), ((), ())),
                preferred_element_type=F32,
            ).astype(BF16)
            for q in range(quarter // SL):
                k = n * (quarter // SL) + q
                for j in range(J):
                    U[j * SL : (j + 1) * SL, k * O : (k + 1) * O] = made[
                        q * SL : (q + 1) * SL, j * O : (j + 1) * O
                    ]
        grT[g] = (
            lax.dot_general(WF[...], U[...], (((1,), (1,)), ((), ())), preferred_element_type=F32) * (1.0 / S)
        ).astype(BF16)
        wacc[...] += jnp.dot(rall[g], U[...], preferred_element_type=F32)

        @pl.when(i == 0)
        def _():
            forward_core()

        @pl.when(i == 1)
        def _():
            finish_gather(near, 0)
            second.wait_recv()
            ycp.wait_recv()
            for h in range(R):
                cut = slice(h * H, (h + 1) * H)
                xsrc[h] = (
                    gl[d, :, cut].astype(F32) + cbuf[0, :, cut].astype(F32) + ybuf[:, cut].astype(F32)
                ).astype(BF16)
            ownx.start()
            for cp in xcps:
                cp.start()

        @pl.when(i == 2)
        def _():
            finish_gather(nearfar, 2)
            ownx.wait()
            for m in range(1, R):
                arrived(Zp.at[lax.rem(r - m + R, R)], bxr.at[m])
            for cp in zcps:
                cp.start()

        return carry

    def sum_left():
            total = Zp[c // ratio, rows(lax.rem(c, ratio) * NI, NI), :].astype(F32)
            for k in range(1, C):
                zcps[k - 1].wait_recv()
                total = total + zin[k - 1].astype(F32)
            fin[...] = total.astype(BF16)
            ownf.start()
            for cp in fcps:
                cp.start()

    lax.fori_loop(0, D, right_grad, 0)

    share, pad = wsum.shape[0], bout.shape[0]
    cuts = CH // share
    scale = 1.0 / (S * crop)
    row = jnp.broadcast_to(bias, (pad, O)).astype(BF16)
    for k in range(CH):
        for p in range(cuts):
            wv[k * cuts + p, 0:share] = (
                wacc[p * share : (p + 1) * share, k * O : (k + 1) * O] * scale
            ).astype(BF16)
            wv[k * cuts + p, share : share + pad] = row

    def spread(k, carry):
        t = lax.rem(me + k, N)
        remote(wv.at[t], win.at[me], ws, wr, place(t)).start()
        return carry

    lax.fori_loop(1, N, spread, 0)
    ownw = pltpu.make_async_copy(wv.at[me], win.at[me], ls.at[0])
    ownw.start()
    for k in range(1, RD):
        t = lax.rem(slot + k, RD)
        launch(
            remote(grT.at[lax.rem(t, D)], grin.at[slot], gs.at[k], grr.at[k], (t // D, c, lax.rem(t, D)))
        )
    owng = pltpu.make_async_copy(grT.at[d], grin.at[slot], ls.at[1])
    owng.start()
    most = win.at[pl.ds(0, N - 1)]
    ownv = pltpu.make_async_copy(wsum, wout.at[me], ls.at[3])

    def publish(k, carry):
        remote(wsum, wout.at[me], vs, vr, place(lax.rem(me + k, N))).start()
        return carry

    def sum_weights():
        ownw.wait()
        arrived(most, wr)
        total = win[0].astype(F32)
        for k in range(1, N):
            total = total + win[k].astype(F32)
        wsum[...] = total[:share].astype(BF16)
        bout[...] = total[share:]
        lax.fori_loop(1, N, publish, 0)
        ownv.start()

    wide = 4 * O if J % 4 == 0 else O
    offset = jnp.concatenate([off[...]] * (wide // O), axis=1)

    half = (J * O // wide) // 2

    def pair_block(n, carry):
        cut = lanes(n * wide, wide)
        made = jnp.dot(L[0], T[0, :, cut], preferred_element_type=F32)
        for g in range(1, D):
            made = made + jnp.dot(L[g], T[g, :, cut], preferred_element_type=F32)
        pair[:, cut] = (made * (1.0 / S) + offset).astype(BF16)
        pl.when(n == half)(sum_weights)
        pl.when(n == J * O // wide - 1)(sum_left)
        return carry

    lax.fori_loop(0, J * O // wide, pair_block, 0)

    owng.wait()
    for k in range(1, RD):
        arrived(grin.at[lax.rem(slot - k + RD, RD)], grr.at[k])
    for q in range(D):
        total = grin[q].astype(F32)
        for h in range(1, R):
            total = total + grin[h * D + q].astype(F32)
        grout[q] = total.astype(BF16)
    ownf.wait()
    for m in range(1, R):
        arrived(glout.at[:, lanes(lax.rem(r - m + R, R) * H, H)], fr.at[m])
    settle_gather()
    first.wait_send()
    second.wait_send()
    ycp.wait_send()
    for cp in sends:
        cp.wait_send()
    arrived(most, ws)
    ownv.wait()
    most = wout.at[pl.ds(0, N - 1)]
    arrived(most, vr)
    arrived(most, vs)


VM = pl.BlockSpec(memory_space=pltpu.VMEM)


def body(alignment_matrix, twin_linear_matrix, final_matrix, final_offset, adjoint_incoming):
    SL, NI, _ = alignment_matrix.shape
    CH = twin_linear_matrix.shape[1] // 2
    O = final_matrix.shape[1]
    R, C, D = lax.axis_size("row"), lax.axis_size("col"), lax.axis_size("depth")
    N = R * C * D
    S = SL * D
    crop = NI * C
    block_i, J, _ = adjoint_incoming.shape
    ratio = C // R
    W = CH * SL
    H = W // R
    DMA = pltpu.SemaphoreType.DMA
    standardized, backprop = jax.vjp(standardize_channels, alignment_matrix.astype(F32))
    normed = standardized.astype(BF16)
    panels = jnp.dot(normed, twin_linear_matrix, preferred_element_type=F32).astype(BF16)
    lt = jnp.transpose(panels[..., :CH], (1, 2, 0)).reshape(NI, W)
    rt = jnp.transpose(panels[..., CH:].reshape(SL, D, J, CH), (1, 3, 2, 0)).reshape(D, CH, J * SL)
    WF = jnp.transpose(final_matrix.reshape(CH, CH, O), (1, 0, 2)).reshape(CH, CH * O)
    A = adjoint_incoming.reshape(block_i, J * O)
    share = CH * CH // N
    pad = 16
    JS = J * SL

    def vb(*shape):
        return pltpu.VMEM(shape, BF16)

    pair, glout, grout, wout, bout = pl.pallas_call(
        functools.partial(fused_kernel, R, C, D, crop),
        out_shape=(
            jax.ShapeDtypeStruct((block_i, J * O), BF16),
            jax.ShapeDtypeStruct((NI, W), BF16),
            jax.ShapeDtypeStruct((D, CH, JS), BF16),
            jax.ShapeDtypeStruct((N, share, O), BF16),
            jax.ShapeDtypeStruct((pad, O), F32),
        ),
        in_specs=[VM] * 5,
        out_specs=(VM,) * 5,
        scratch_shapes=[
            vb(D, block_i, W), vb(D, CH, JS), vb(D, W, J * O), vb(JS, CH * O), vb(D, block_i, W),
            vb(D, CH, JS), pltpu.VMEM((CH, CH * O), F32), vb(C, NI, H), vb(2, block_i, W),
            vb(block_i, W), vb(block_i, W), vb(R, block_i, H), vb(R, block_i, H), vb(C - 1, NI, H),
            vb(NI, H), vb(R * D, CH, JS), vb(N, share + pad, O), vb(N, share + pad, O), vb(share, O),
            DMA((C,)), DMA((C,)), DMA((R, ratio)), DMA((R, ratio)),
            DMA((3, R, ratio)), DMA((3, R, ratio)), DMA((D,)), DMA((D,)), DMA((ratio,)),
            DMA((2,)), DMA((2,)), DMA, DMA, DMA((R,)), DMA((R,)), DMA((C,)), DMA((C,)),
            DMA((R,)), DMA((R,)), DMA((R * D,)), DMA((R * D,)), DMA, DMA, DMA, DMA, DMA((5,)),
        ],
        compiler_params=pltpu.CompilerParams(
            collective_id=0, has_side_effects=True, vmem_limit_bytes=63 * 1024 * 1024
        ),
        name="pair_and_exchange",
    )(lt, rt, A, WF, final_offset.reshape(1, O))
    contact_delta = pair.reshape(block_i, J, O)
    left = jnp.transpose(glout.reshape(NI, CH, SL), (2, 0, 1))
    right = jnp.transpose(grout.reshape(D, CH, J, SL), (3, 0, 2, 1)).reshape(SL, NI, CH)
    grad_panels = jnp.concatenate([left, right], axis=-1)
    adjoint = jnp.einsum("slk,mk->slm", grad_panels, twin_linear_matrix, preferred_element_type=F32)
    return (
        contact_delta,
        backprop(adjoint)[0],
        wout.reshape(CH * CH, O).astype(F32),
        bout[0],
    )


def solution(mesh):
    in_specs = (P("depth", "col", None), P(), P(), P(), P("row", ("col", "depth"), None))
    out_specs = (P("row", ("col", "depth"), None), P("depth", "col", None), P(), P())
    return jax.shard_map(body, mesh=mesh, in_specs=in_specs, out_specs=out_specs, check_vma=False)
```
